256 devices in a mesh: ep: 64 (over z, x, core), tp: 4 (over y).
Axes of the slice: x: 4, y: 4, z: 8, core: 2. Of those that a mesh axis runs over, the one named last changes fastest.
Arguments:
- tokens: bfloat16 [16384, 3584], P('ep', 'tp'), may hold values from -6 to 6
- grad_out: bfloat16 [16384, 3584], P('ep', 'tp'), may hold values from -6 to 6
- route_ids: int32 [16384, 2], P('ep'), may hold values from 0 to 63, all different within a row; in each aligned block of 256 rows (0 to 255, 256 to 511, ...) at most 16 rows name the same one
- route_probs: float32 [16384, 2], P('ep'), may hold values from 0.2 to 1
- w_gate: bfloat16 [64, 3584, 1024], P('ep', None, 'tp'), may hold values from -0.09375 to 0.09375
- w_up: bfloat16 [64, 3584, 1024], P('ep', None, 'tp'), may hold values from -0.09375 to 0.09375
- w_down: bfloat16 [64, 1024, 3584], P('ep', 'tp'), may hold values from -0.1875 to 0.1875
Outputs:
- grad_tokens: bfloat16 [16384, 3584], P('ep', 'tp')
- grad_gate: bfloat16 [64, 3584, 1024], P('ep', None, 'tp')
- grad_up: bfloat16 [64, 3584, 1024], P('ep', None, 'tp')
- grad_down: bfloat16 [64, 1024, 3584], P('ep', 'tp')
The draws below stay inside these ranges and needn't reach their ends.
Inputs may be any that keep to these rules, and one draw needn't show every extreme that they name: `route_ids`: each token names 2 different experts. Among the tokens of one index of ep (aligned blocks of 256 tokens), no expert is named by more than 16 tokens, and in every draw some expert is named by exactly 16 of some block.
All inputs are finite; a program needn't handle non-finite values.
Results may differ from the reference program's by a relative error of at most 0.0065.
Values may be sent and summed in bfloat16 or wider, within the bound.
No kernel may reach another device: no remote copies, remote signals or barrier semaphores. Data moves between devices by JAX's collectives and lax.ppermute only.
A program may use at most 128 MiB of HBM per device.

```python
import math
import jax
import jax.numpy as jnp
import numpy as np
from jax import lax

D = 3584
FF = 1024
TOP = 2
TOK_DEV = 256
TOKENS = 16384
EXPERTS = 64
CAP = 16
N_EP = 64


def shard_levels(rng, dims, pieces, low, high):
    def one(position, parts):
        heights = jax.random.uniform(jax.random.fold_in(jax.random.fold_in(rng, 6), position), (parts,), jnp.float32, low / len(pieces), high / len(pieces))
        return jnp.repeat(jnp.exp(heights), dims[position] // parts).reshape((-1,) + (1,) * (len(dims) - position - 1))

    gain = one(*pieces[0])
    for cut in pieces[1:]:
        gain = gain * one(*cut)
    return gain


def deal_out(key, own, number, rows, number_of, top, most, slope):
    sequence = jax.random.permutation(key, number_of)
    heavy_load, common = shares(number_of, rows * top, most, slope, True), shares(number_of, rows * top, most, slope, False)
    places = jnp.arange(number_of)

    def named(lengths, offset_by):
        used = int((lengths > 0).sum())
        fixed = max(1, used // 4)
        passed = fixed + (places - fixed + offset_by * (used - fixed)) % max(1, number_of - fixed)
        return jnp.zeros((number_of,), jnp.int32).at[sequence[jnp.where(places < fixed, places, passed)]].set(jnp.asarray(lengths, jnp.int32))

    lengths = jnp.where(number % 4 == 0, named(heavy_load, number // 4), named(common, number - number // 4 - 1))
    mixed = jax.random.permutation(jax.random.fold_in(own, 3), number_of)
    giver, sink = mixed[0:number_of // 2 * 2:2], mixed[1:number_of // 2 * 2:2]
    room = jnp.minimum(lengths[giver] - 1, most - lengths[sink]) // 2
    room = jnp.where((giver == sequence[0]) | (sink == sequence[0]) | (lengths[sink] == 0), 0, jnp.maximum(room, 0))
    passed = jax.random.randint(jax.random.fold_in(own, 4), (number_of // 2,), 0, 1 << 20) % (room + 1)
    lengths = lengths.at[giver].add(-passed).at[sink].add(passed)
    members = jnp.searchsorted(jnp.cumsum(lengths), jnp.arange(rows * top), side="right").astype(jnp.int32)
    listing = members.reshape(top, rows).T
    listing = listing[jax.random.permutation(jax.random.fold_in(own, 1), rows)]
    offset_by = jax.random.randint(jax.random.fold_in(own, 2), (rows, 1), 0, top)
    return jnp.take_along_axis(listing, (jnp.arange(top)[None, :] + offset_by) % top, axis=1)


def shares(count, total, bound, skew, full):
    weights = [(1 << 20) // math.isqrt(rank ** skew) + 1 for rank in range(1, count + 1)]
    largest = bound if full else min(bound, max(-(-total // count), total * weights[0] // sum(weights)))
    least = 1 if total - largest >= count - 1 else 0
    holding, rest = [largest] + [least] * (count - 1), total - largest - least * (count - 1)
    while rest > 0:
        movable = [i for i in range(1, count) if holding[i] < largest] or [i for i in range(1, count) if holding[i] < bound]
        mass, remaining = sum([weights[i] for i in movable]), rest
        for i in movable:
            addition = min(bound - holding[i], max(1, remaining * weights[i] // mass), rest)
            holding[i] = holding[i] + addition
            rest = rest - addition
    return np.array(holding)


def bell_draw(key, extent, spread, bound, split=(), kind=jnp.bfloat16):
    result = spread * jax.random.normal(key, extent, jnp.float32)
    if split:
        result = result * shard_levels(key, extent, split, -0.22, 0.18)
    return jnp.clip(result, -bound, bound).astype(kind)


def setup_inputs(seed: int = 0) -> dict:
    key_of = jax.random.split(jax.random.key(seed), 8)
    tokens = bell_draw(key_of[0], (TOKENS, D), 1.0, 6.0, ((0, 64), (1, 4)))
    grad_out = bell_draw(key_of[1], (TOKENS, D), 1.0, 6.0, ((0, 64), (1, 4)))
    route_ids_keys = jax.random.split(jax.random.fold_in(key_of[2], 1), TOKENS // TOK_DEV)
    route_ids_turns = jax.random.permutation(jax.random.fold_in(key_of[2], 3), TOKENS // TOK_DEV)
    route_ids = jax.vmap(lambda own, number: deal_out(jax.random.fold_in(key_of[2], 2), own, number, TOK_DEV, EXPERTS, TOP, CAP, 1))(route_ids_keys, route_ids_turns).reshape((TOKENS, TOP))
    route_probs = jnp.clip(0.2 + 0.8 * jax.random.uniform(key_of[3], (TOKENS, TOP), jnp.float32) ** shard_levels(key_of[3], (TOKENS, TOP), ((0, 64),), -0.2, 0.2), 0.2, 1.0)
    w_gate = bell_draw(key_of[4], (EXPERTS, D, FF), D ** -0.5, 0.09375, ((0, 64), (2, 4)))
    w_up = bell_draw(key_of[5], (EXPERTS, D, FF), D ** -0.5, 0.09375, ((0, 64), (2, 4)))
    w_down = bell_draw(key_of[6], (EXPERTS, FF, D), FF ** -0.5, 0.1875, ((0, 64), (1, 4)))
    return {"tokens": tokens, "grad_out": grad_out, "route_ids": route_ids, "route_probs": route_probs, "w_gate": w_gate, "w_up": w_up, "w_down": w_down}


def contract_last(left, right):
    return lax.dot_general(left, right, (((1,), (1,)), ((), ())), preferred_element_type=jnp.float32)


def contract_first(left, right):
    return lax.dot_general(left, right, (((0,), (0,)), ((), ())), preferred_element_type=jnp.float32)


def row_pass(x_rows, s_rows, gate_cols, up_cols, down_rows):
    gate = jnp.dot(x_rows, gate_cols, preferred_element_type=jnp.float32)
    upper = jnp.dot(x_rows, up_cols, preferred_element_type=jnp.float32)
    sigma = jax.nn.sigmoid(gate)
    active = gate * sigma
    hidden = (active * upper).astype(jnp.bfloat16)
    back = contract_last(s_rows, down_rows)
    d_up = (back * active).astype(jnp.bfloat16)
    d_gate = (back * upper * sigma * (1.0 + gate * (1.0 - sigma))).astype(jnp.bfloat16)
    return d_gate, d_up, contract_first(x_rows, d_gate), contract_first(x_rows, d_up), contract_first(hidden, s_rows)


def reference(tokens, grad_out, route_ids, route_probs, w_gate, w_up, w_down):
    routes = TOKENS * TOP
    rows_e = N_EP * CAP
    flat_ids = route_ids.reshape(-1).astype(jnp.int32)
    onehot = (flat_ids[:, None] == jnp.arange(EXPERTS, dtype=jnp.int32)[None, :]).astype(jnp.int32)
    rank = jnp.sum((jnp.cumsum(onehot, axis=0) - onehot) * onehot, axis=1).astype(jnp.int32)
    table = jnp.full((EXPERTS * rows_e,), routes, dtype=jnp.int32)
    table = table.at[flat_ids * rows_e + rank].set(jnp.arange(routes, dtype=jnp.int32))
    flat_probs = route_probs.reshape(-1)

    def per_expert(total, expert):
        index = lax.dynamic_slice_in_dim(table, expert * rows_e, rows_e)
        live = index < routes
        token = jnp.where(live, index // TOP, TOKENS).astype(jnp.int32)
        x_rows = jnp.take(tokens, token, axis=0, mode="fill", fill_value=0)
        prob = jnp.where(live, jnp.take(flat_probs, jnp.where(live, index, 0).astype(jnp.int32)), 0.0)
        dy_rows = jnp.take(grad_out, token, axis=0, mode="fill", fill_value=0).astype(jnp.float32)
        s_rows = (prob[:, None] * dy_rows).astype(jnp.bfloat16)
        d_gate, d_up, g_gate, g_up, g_down = row_pass(x_rows, s_rows, w_gate[expert], w_up[expert], w_down[expert])
        route_dx = (contract_last(d_gate, w_gate[expert]) + contract_last(d_up, w_up[expert])).astype(jnp.bfloat16)
        total = total.at[token].add(route_dx.astype(jnp.float32), mode="drop")
        return total, (g_gate.astype(jnp.bfloat16), g_up.astype(jnp.bfloat16), g_down.astype(jnp.bfloat16))

    total, grads = lax.scan(per_expert, jnp.zeros((TOKENS, D), jnp.float32), jnp.arange(EXPERTS, dtype=jnp.int32))
    return total.astype(jnp.bfloat16), grads[0], grads[1], grads[2]
```

```python
import jax
import jax.numpy as jnp
from jax import lax
from jax.sharding import PartitionSpec as P


CHUNKS = 2
BF = jnp.bfloat16
F32 = jnp.float32


def mm(left, right, dims):
    return lax.dot_general(left, right, (dims, ((), ())), preferred_element_type=F32)


def per_device(tokens, grad_out, route_ids, route_probs, w_gate, w_up, w_down):
    n_src = lax.axis_size("ep")
    n_tp = lax.axis_size("tp")
    me = lax.axis_index("tp")
    tok_rows, quarter = tokens.shape
    top = route_ids.shape[1]
    cap = max(2, 2 * tok_rows * top // n_src)
    part = cap // CHUNKS
    rows = n_src * part
    hid = w_gate.shape[2]
    shifts = range(1, n_tp)

    def fetch(a, k):
        return lax.ppermute(a, "tp", [((i + k) % n_tp, i) for i in range(n_tp)])

    def give(a, k):
        return lax.ppermute(a, "tp", [(i, (i + k) % n_tp) for i in range(n_tp)])

    def exchange(a):
        return lax.all_to_all(
            a.reshape(n_src, part, quarter), "ep", split_axis=0, concat_axis=0, tiled=True
        ).reshape(rows, quarter)

    ids = route_ids.T
    probs = route_probs.T
    experts = lax.broadcasted_iota(jnp.int32, (n_src, tok_rows), 0)
    hot = [experts == ids[k : k + 1] for k in range(top)]
    named = sum(h.astype(BF) for h in hot)
    before = (
        lax.broadcasted_iota(jnp.int32, (tok_rows, tok_rows), 0)
        < lax.broadcasted_iota(jnp.int32, (tok_rows, tok_rows), 1)
    ).astype(BF)
    earlier = mm(named, before, ((1,), (0,)))
    rank = [
        jnp.sum(jnp.where(h, earlier, 0.0), axis=0, keepdims=True).astype(jnp.int32) for h in hot
    ]
    row_index = lax.broadcasted_iota(jnp.int32, (rows, tok_rows), 0)
    picks = []
    for c in range(CHUNKS):
        found = []
        for k in range(top):
            place = rank[k] - c * part
            inside = (place >= 0) & (place < part)
            found.append(row_index == jnp.where(inside, ids[k : k + 1] * part + place, -1))
        picks.append(found)
    pick = [sum(f.astype(BF) for f in found) for found in picks]

    gate_q = w_gate[0].reshape(n_tp, quarter, hid)
    up_q = w_up[0].reshape(n_tp, quarter, hid)
    down = w_down[0]

    def at(a, k):
        return lax.dynamic_index_in_dim(a, lax.rem(me + k, n_tp), 0, keepdims=False)

    def down_at(k):
        start = lax.rem(me + k, n_tp) * quarter
        return lax.dynamic_slice_in_dim(down, start, quarter, axis=1)


    x_send = [mm(p, tokens, ((1,), (0,))).astype(BF) for p in pick]
    x_own = [exchange(a) for a in x_send]
    s_send = []
    for c in range(CHUNKS):
        weight = sum(
            jnp.sum(jnp.where(picks[c][k], probs[k : k + 1], 0.0), axis=1, keepdims=True)
            for k in range(top)
        )
        s_send.append((mm(pick[c], grad_out, ((1,), (0,))) * weight).astype(BF))
    s_own = [exchange(a) for a in s_send]

    back_w = [down_at(0)] + [fetch(down_at(n_tp - k), k) for k in shifts]
    both = [jnp.concatenate([at(gate_q, n_tp - k), at(up_q, n_tp - k)], axis=1) for k in range(n_tp)]
    dx_w = [both[0]] + [fetch(both[k], k) for k in shifts]

    x_all = [[x] + [fetch(x, k) for k in shifts] for x in x_own]
    acts = []
    for c in range(CHUNKS):
        gate = sum(mm(x_all[c][k], at(gate_q, k), ((1,), (0,))) for k in range(n_tp))
        upper = sum(mm(x_all[c][k], at(up_q, k), ((1,), (0,))) for k in range(n_tp))
        acts.append((gate, upper))

    d_own, hidden = [], []
    for c in range(CHUNKS):
        terms = [mm(s_own[c], back_w[k], ((1,), (1,))) for k in range(n_tp)]
        back = terms[0] + sum(give(terms[k].astype(BF), k).astype(F32) for k in shifts)
        gate, upper = acts[c]
        sigma = jax.nn.sigmoid(gate)
        active = gate * sigma
        hidden.append((active * upper).astype(BF))
        d_up = (back * active).astype(BF)
        d_gate = (back * upper * sigma * (1.0 + gate * (1.0 - sigma))).astype(BF)
        d_own.append(jnp.concatenate([d_gate, d_up], axis=1))
    dx_back = []
    for c in range(CHUNKS):
        d_all = [d_own[c]] + [fetch(d_own[c], k) for k in shifts]
        dx = sum(mm(d_all[k], dx_w[k], ((1,), (1,))) for k in range(n_tp))
        dx_back.append(exchange(dx.astype(BF)))

    grad_tokens = sum(
        mm(pick[c], dx_back[c], ((0,), (0,))) for c in range(CHUNKS)
    ).astype(BF)

    g_gate = jnp.zeros((n_tp, quarter, hid), BF)
    g_up = jnp.zeros((n_tp, quarter, hid), BF)
    for k in range(n_tp):
        both_g = sum(mm(x_all[c][k], d_own[c], ((0,), (0,))) for c in range(CHUNKS)).astype(BF)
        spot = lax.rem(me + k, n_tp)
        g_gate = lax.dynamic_update_index_in_dim(g_gate, both_g[:, :hid], spot, 0)
        g_up = lax.dynamic_update_index_in_dim(g_up, both_g[:, hid:], spot, 0)

    h_all = [[h] + [fetch(h, k) for k in shifts] for h in hidden]
    g_down = jnp.zeros(down.shape, BF)
    for k in range(n_tp):
        piece = sum(mm(h_all[c][k], s_own[c], ((0,), (0,))) for c in range(CHUNKS)).astype(BF)
        if k:
            piece = give(piece, k)
        spot = lax.rem(me + n_tp - k, n_tp)
        g_down = lax.dynamic_update_slice_in_dim(g_down, piece, spot * quarter, axis=1)

    return (
        grad_tokens,
        g_gate.reshape(1, n_tp * quarter, hid),
        g_up.reshape(1, n_tp * quarter, hid),
        g_down[None],
    )


def solution(mesh):
    placed = (
        P("ep", "tp"),
        P("ep", "tp"),
        P("ep", None),
        P("ep", None),
        P("ep", None, "tp"),
        P("ep", None, "tp"),
        P("ep", "tp", None),
    )

    return jax.shard_map(
        per_device,
        mesh=mesh,
        in_specs=placed,
        out_specs=(P("ep", "tp"), P("ep", None, "tp"), P("ep", None, "tp"), P("ep", "tp", None)),
        check_vma=False,
    )
```

```python
import jax
import jax.numpy as jnp
from jax import lax
from jax.sharding import PartitionSpec as P


CHUNKS = 2
BF = jnp.bfloat16
F32 = jnp.float32


def mm(left, right, dims):
    return lax.dot_general(left, right, (dims, ((), ())), preferred_element_type=F32)


def per_device(tokens, grad_out, route_ids, route_probs, w_gate, w_up, w_down):
    n_src = lax.axis_size("ep")
    n_tp = lax.axis_size("tp")
    me = lax.axis_index("tp")
    tok_rows, quarter = tokens.shape
    top = route_ids.shape[1]
    cap = max(2, 2 * tok_rows * top // n_src)
    part = cap // CHUNKS
    rows = n_src * cap
    hid = w_gate.shape[2]
    shifts = range(1, n_tp)

    def fetch(a, k):
        return lax.ppermute(a, "tp", [((i + k) % n_tp, i) for i in range(n_tp)])

    def give(a, k):
        return lax.ppermute(a, "tp", [(i, (i + k) % n_tp) for i in range(n_tp)])

    def exchange(a):
        return lax.all_to_all(
            a.reshape(n_src, -1, quarter), "ep", split_axis=0, concat_axis=0, tiled=True
        ).reshape(-1, quarter)

    ids = route_ids.T
    probs = route_probs.T
    experts = lax.broadcasted_iota(jnp.int32, (n_src, tok_rows), 0)
    hot = [experts == ids[k : k + 1] for k in range(top)]
    named = sum(h.astype(BF) for h in hot)
    before = (
        lax.broadcasted_iota(jnp.int32, (tok_rows, tok_rows), 0)
        < lax.broadcasted_iota(jnp.int32, (tok_rows, tok_rows), 1)
    ).astype(BF)
    earlier = mm(named, before, ((1,), (0,)))
    rank = [
        jnp.sum(jnp.where(h, earlier, 0.0), axis=0, keepdims=True).astype(jnp.int32) for h in hot
    ]

    def picks_of(first, count):
        row_index = lax.broadcasted_iota(jnp.int32, (n_src * count, tok_rows), 0)
        found = []
        for k in range(top):
            place = rank[k] - first
            inside = (place >= 0) & (place < count)
            found.append(row_index == jnp.where(inside, ids[k : k + 1] * count + place, -1))
        return found

    found = picks_of(0, cap)
    pick = sum(f.astype(BF) for f in found)

    gate_q = w_gate[0].reshape(n_tp, quarter, hid)
    up_q = w_up[0].reshape(n_tp, quarter, hid)
    down = w_down[0]

    def at(a, k):
        return lax.dynamic_index_in_dim(a, lax.rem(me + k, n_tp), 0, keepdims=False)

    def down_at(k):
        start = lax.rem(me + k, n_tp) * quarter
        return lax.dynamic_slice_in_dim(down, start, quarter, axis=1)

    x_own = exchange(mm(pick, tokens, ((1,), (0,))).astype(BF))
    weight = sum(
        jnp.sum(jnp.where(found[k], probs[k : k + 1], 0.0), axis=1, keepdims=True)
        for k in range(top)
    )
    s_own = exchange((mm(pick, grad_out, ((1,), (0,))) * weight).astype(BF))

    back_w = [down_at(0)] + [fetch(down_at(n_tp - k), k) for k in shifts]
    both = [jnp.concatenate([at(gate_q, n_tp - k), at(up_q, n_tp - k)], axis=1) for k in range(n_tp)]
    dx_w = [both[0]] + [fetch(both[k], k) for k in shifts]

    half = rows // 2
    x_next, x_last = fetch(x_own, 1), fetch(x_own, n_tp - 1)
    x_far = jnp.concatenate([fetch(x_next[:half], 1), fetch(x_last[half:], n_tp - 1)], axis=0)
    x_all = [x_own, x_next, x_far, x_last]
    gate = sum(mm(x_all[k], at(gate_q, k), ((1,), (0,))) for k in range(n_tp))
    upper = sum(mm(x_all[k], at(up_q, k), ((1,), (0,))) for k in range(n_tp))

    terms = [mm(s_own, back_w[k], ((1,), (1,))) for k in range(n_tp)]
    back = terms[0] + sum(give(terms[k].astype(BF), k).astype(F32) for k in shifts)
    sigma = jax.nn.sigmoid(gate)
    active = gate * sigma
    hidden = (active * upper).astype(BF)
    d_up = (back * active).astype(BF)
    d_gate = (back * upper * sigma * (1.0 + gate * (1.0 - sigma))).astype(BF)
    d_own = jnp.concatenate([d_gate, d_up], axis=1)

    grad_tokens = 0.0
    for c in range(CHUNKS):
        d_part = d_own.reshape(n_src, cap, 2 * hid)[:, c * part : (c + 1) * part]
        d_part = d_part.reshape(n_src * part, 2 * hid)
        d_all = [d_part] + [fetch(d_part, k) for k in shifts]
        dx = mm(d_part, dx_w[0], ((1,), (1,)))
        dx += sum(mm(d_all[k], dx_w[k], ((1,), (1,))) for k in shifts)
        dx = exchange(dx.astype(BF))
        spots = sum(f.astype(BF) for f in picks_of(c * part, part))
        grad_tokens += mm(spots, dx, ((0,), (0,)))
    grad_tokens = grad_tokens.astype(BF)

    g_gate = jnp.zeros((n_tp, quarter, hid), BF)
    g_up = jnp.zeros((n_tp, quarter, hid), BF)
    for k in range(n_tp):
        both_g = mm(x_all[k], d_own, ((0,), (0,))).astype(BF)
        spot = lax.rem(me + k, n_tp)
        g_gate = lax.dynamic_update_index_in_dim(g_gate, both_g[:, :hid], spot, 0)
        g_up = lax.dynamic_update_index_in_dim(g_up, both_g[:, hid:], spot, 0)

    h_all = [hidden] + [fetch(hidden, k) for k in shifts]
    g_down = jnp.zeros(down.shape, BF)
    for k in range(n_tp):
        piece = mm(h_all[k], s_own, ((0,), (0,))).astype(BF)
        if k:
            piece = give(piece, k)
        spot = lax.rem(me + n_tp - k, n_tp)
        g_down = lax.dynamic_update_slice_in_dim(g_down, piece, spot * quarter, axis=1)

    return (
        grad_tokens,
        g_gate.reshape(1, n_tp * quarter, hid),
        g_up.reshape(1, n_tp * quarter, hid),
        g_down[None],
    )


def solution(mesh):
    placed = (
        P("ep", "tp"),
        P("ep", "tp"),
        P("ep", None),
        P("ep", None),
        P("ep", None, "tp"),
        P("ep", None, "tp"),
        P("ep", "tp", None),
    )

    return jax.shard_map(
        per_device,
        mesh=mesh,
        in_specs=placed,
        out_specs=(P("ep", "tp"), P("ep", None, "tp"), P("ep", None, "tp"), P("ep", "tp", None)),
        check_vma=False,
    )
```

```python
import jax
import jax.numpy as jnp
from jax import lax
from jax.experimental import pallas as pl
from jax.experimental.pallas import tpu as pltpu
from jax.sharding import PartitionSpec as P


TILES = 4
BF = jnp.bfloat16
F32 = jnp.float32


def mm(left, right, dims):
    return lax.dot_general(left, right, (dims, ((), ())), preferred_element_type=F32)


def rows_by_columns(left, right):
    return mm(left, right, ((1,), (0,)))


def pack_kernel(me, gate, up, down, *packed):
    n = len(packed)
    quarter, hid = gate.shape[1:]
    for k in range(n):
        out = packed[k]
        q = lax.rem(me[0] + n - k, n)

        @pl.loop(0, quarter // 128)
        def _(t):
            span = pl.ds(pl.multiple_of(t * 128, 128), 128)
            out[span, 0:hid] = gate[q, span, :]
            out[span, hid : 2 * hid] = up[q, span, :]
            start = pl.multiple_of(q * quarter + t * 128, 128)
            out[span, 2 * hid : 3 * hid] = down[:, pl.ds(start, 128)].T


def partial_kernel(me, own, after, last, gate, up, out):
    n, _, hid = gate.shape
    pieces = ((own, 0), (after, 1), (last, n - 1))
    for weight, first in ((gate, 0), (up, hid)):
        out[:, first : first + hid] = sum(
            rows_by_columns(x[...], weight[lax.rem(me[0] + k, n)]) for x, k in pieces
        )


def back_kernel(s, *refs):
    n = len(refs) // 2
    for k in range(n):
        out = refs[n + k]
        out[...] = rows_by_columns(s[...], refs[k][...]).astype(out.dtype)


def acts_kernel(me, far_a, far_b, partial, gate_w, up_w, *refs):
    hidden, grads, x = refs[-3:]
    step = pl.program_id(0)

    @pl.when(step < TILES // 2)
    def _():
        x[...] = far_a[...]

    @pl.when(step >= TILES // 2)
    def _():
        x[...] = far_b[...]

    hid = gate_w.shape[2]
    gate = partial[:, :hid] + rows_by_columns(x[...], gate_w[0])
    upper = partial[:, hid:] + rows_by_columns(x[...], up_w[0])
    back = sum(r[...].astype(F32) for r in refs[:-3])
    sigma = jax.nn.sigmoid(gate)
    active = gate * sigma
    hidden[...] = (active * upper).astype(BF)
    grads[:, :hid] = (back * upper * sigma * (1.0 + gate * (1.0 - sigma))).astype(BF)
    grads[:, hid:] = (back * active).astype(BF)


def dx_kernel(*refs):
    n = len(refs) // 2
    total = mm(refs[0][...], refs[n][...], ((1,), (1,)))
    for k in range(1, n):
        total += mm(refs[k][...], refs[n + k][...], ((1,), (1,)))
    refs[-1][...] = total.astype(BF)


def call(kernel, scalars, ins, outs, grid, scratch, flops, operands):
    moved = sum(a.size * a.dtype.itemsize for a in operands)
    return pl.pallas_call(
        kernel,
        out_shape=[s for s, _ in outs],
        grid_spec=pltpu.PrefetchScalarGridSpec(
            num_scalar_prefetch=scalars,
            grid=grid,
            in_specs=ins,
            out_specs=[b for _, b in outs],
            scratch_shapes=scratch,
        ),
        cost_estimate=pl.CostEstimate(flops=flops, bytes_accessed=moved, transcendentals=0),
    )(*operands)


def per_device(tokens, grad_out, route_ids, route_probs, w_gate, w_up, w_down):
    n_src = lax.axis_size("ep")
    n_tp = lax.axis_size("tp")
    me = lax.axis_index("tp")
    spot = me.astype(jnp.int32).reshape(1)
    tok_rows, quarter = tokens.shape
    top = route_ids.shape[1]
    cap = max(2, 2 * tok_rows * top // n_src)
    rows = n_src * cap
    tile = rows // TILES
    hid = w_gate.shape[2]
    shifts = range(1, n_tp)

    def fetch(a, k):
        return lax.ppermute(a, "tp", [((i + k) % n_tp, i) for i in range(n_tp)])

    def give(a, k):
        return lax.ppermute(a, "tp", [(i, (i + k) % n_tp) for i in range(n_tp)])

    def exchange(a):
        return lax.all_to_all(
            a.reshape(n_src, cap, quarter), "ep", split_axis=0, concat_axis=0, tiled=True
        ).reshape(rows, quarter)

    def by_rows(width):
        return pl.BlockSpec((tile, width), lambda i, *_: (i, 0))

    def whole(shape):
        return pl.BlockSpec(shape, lambda *_: (0,) * len(shape))

    def array(shape, kind):
        return jax.ShapeDtypeStruct(shape, kind)

    ids = route_ids.T
    probs = route_probs.T
    experts = lax.broadcasted_iota(jnp.int32, (n_src, tok_rows), 0)
    hot = [experts == ids[k : k + 1] for k in range(top)]
    named = sum(h.astype(BF) for h in hot)
    before = (
        lax.broadcasted_iota(jnp.int32, (tok_rows, tok_rows), 0)
        < lax.broadcasted_iota(jnp.int32, (tok_rows, tok_rows), 1)
    ).astype(BF)
    earlier = rows_by_columns(named, before)
    row_index = lax.broadcasted_iota(jnp.int32, (rows, tok_rows), 0)
    found = []
    for k in range(top):
        rank = jnp.sum(jnp.where(hot[k], earlier, 0.0), axis=0, keepdims=True).astype(jnp.int32)
        found.append(row_index == ids[k : k + 1] * cap + rank)
    pick = sum(f.astype(BF) for f in found)

    x_own = exchange(rows_by_columns(pick, tokens).astype(BF))
    weight = sum(
        jnp.sum(jnp.where(found[k], probs[k : k + 1], 0.0), axis=1, keepdims=True)
        for k in range(top)
    )
    s_own = exchange((rows_by_columns(pick, grad_out) * weight).astype(BF))

    gate_q = w_gate[0].reshape(n_tp, quarter, hid)
    up_q = w_up[0].reshape(n_tp, quarter, hid)
    down = w_down[0]
    packed_shape = (quarter, 3 * hid)
    packed = call(
        pack_kernel,
        1,
        [whole(gate_q.shape), whole(up_q.shape), whole(down.shape)],
        [(array(packed_shape, BF), whole(packed_shape))] * n_tp,
        (1,),
        [],
        0,
        (spot, gate_q, up_q, down),
    )
    packed = [packed[0]] + [fetch(packed[k], k) for k in shifts]

    half = rows // 2
    x_next, x_last = fetch(x_own, 1), fetch(x_own, n_tp - 1)
    far_a = fetch(x_next[:half], 1)
    far_b = fetch(x_last[half:], n_tp - 1)
    (partial,) = call(
        partial_kernel,
        1,
        [by_rows(quarter)] * 3 + [whole(gate_q.shape), whole(up_q.shape)],
        [(array((rows, 2 * hid), F32), by_rows(2 * hid))],
        (TILES,),
        [],
        12 * rows * quarter * hid,
        (spot, x_own, x_next, x_last, gate_q, up_q),
    )

    terms = call(
        back_kernel,
        0,
        [by_rows(quarter)] + [pl.BlockSpec((quarter, hid), lambda i: (0, 2))] * n_tp,
        [(array((rows, hid), BF if k else F32), by_rows(hid)) for k in range(n_tp)],
        (TILES,),
        [],
        2 * n_tp * rows * quarter * hid,
        (s_own, *packed),
    )
    terms = [terms[0]] + [give(terms[k], k) for k in shifts]
    mid = TILES // 2
    opposite = pl.BlockSpec((1, quarter, hid), lambda i, m: (lax.rem(m[0] + 2, n_tp), 0, 0))
    hidden, d_own = call(
        acts_kernel,
        1,
        [
            pl.BlockSpec((tile, quarter), lambda i, m: (jnp.minimum(i, mid - 1), 0)),
            pl.BlockSpec((tile, quarter), lambda i, m: (jnp.maximum(i - mid, 0), 0)),
            by_rows(2 * hid),
            opposite,
            opposite,
        ]
        + [by_rows(hid)] * n_tp,
        [(array((rows, hid), BF), by_rows(hid)), (array((rows, 2 * hid), BF), by_rows(2 * hid))],
        (TILES,),
        [pltpu.VMEM((tile, quarter), BF)],
        4 * rows * quarter * hid,
        (spot, far_a, far_b, partial, gate_q, up_q, *terms),
    )
    d_all = [d_own] + [fetch(d_own, k) for k in shifts]
    (dx,) = call(
        dx_kernel,
        0,
        [by_rows(2 * hid)] * n_tp
        + [pl.BlockSpec((quarter, 2 * hid), lambda i: (0, 0))] * n_tp,
        [(array((rows, quarter), BF), by_rows(quarter))],
        (TILES,),
        [],
        4 * n_tp * rows * quarter * hid,
        (*d_all, *packed),
    )
    dx = exchange(dx)
    grad_tokens = mm(pick, dx, ((0,), (0,))).astype(BF)

    x_full = jnp.zeros((rows, n_tp * quarter), BF)
    x_far = jnp.concatenate([far_a, far_b], axis=0)
    for k, piece in ((0, x_own), (1, x_next), (2, x_far), (n_tp - 1, x_last)):
        start = lax.rem(me + k, n_tp) * quarter
        x_full = lax.dynamic_update_slice_in_dim(x_full, piece, start, axis=1)
    g_gate = mm(x_full, d_own[:, :hid], ((0,), (0,))).astype(BF)
    g_up = mm(x_full, d_own[:, hid:], ((0,), (0,))).astype(BF)

    h_all = [hidden] + [fetch(hidden, k) for k in shifts]
    g_down = jnp.zeros(down.shape, BF)
    for k in range(n_tp):
        piece = mm(h_all[k], s_own, ((0,), (0,))).astype(BF)
        if k:
            piece = give(piece, k)
        start = lax.rem(me + n_tp - k, n_tp) * quarter
        g_down = lax.dynamic_update_slice_in_dim(g_down, piece, start, axis=1)

    return grad_tokens, g_gate[None], g_up[None], g_down[None]


def solution(mesh):
    placed = (
        P("ep", "tp"),
        P("ep", "tp"),
        P("ep", None),
        P("ep", None),
        P("ep", None, "tp"),
        P("ep", None, "tp"),
        P("ep", "tp", None),
    )

    return jax.shard_map(
        per_device,
        mesh=mesh,
        in_specs=placed,
        out_specs=(P("ep", "tp"), P("ep", None, "tp"), P("ep", None, "tp"), P("ep", "tp", None)),
        check_vma=False,
    )
```

```python
import jax
import jax.numpy as jnp
from jax import lax
from jax.experimental import pallas as pl
from jax.experimental.pallas import tpu as pltpu
from jax.sharding import PartitionSpec as P


TILES = 4
CHUNKS = 2
BF = jnp.bfloat16
F32 = jnp.float32


def mm(left, right, dims):
    return lax.dot_general(left, right, (dims, ((), ())), preferred_element_type=F32)


def rows_by_columns(left, right):
    return mm(left, right, ((1,), (0,)))


def pack_kernel(me, gate, up, down, *packed):
    n = len(packed)
    step = pl.program_id(0)
    span, hid = gate.shape[1:]
    width = down.shape[1] // n
    for k in range(n):
        q = lax.rem(me[0] + n - k, n)
        packed[k][:, 0:hid] = gate[q]
        packed[k][:, hid : 2 * hid] = up[q]
        start = pl.multiple_of(q * width + step * span, 128)
        packed[k][:, 2 * hid : 3 * hid] = down[:, pl.ds(start, span)].T


def partial_kernel(me, own, after, last, gate, up, out):
    n, _, hid = gate.shape
    pieces = ((own, 0), (after, 1), (last, n - 1))
    for weight, first in ((gate, 0), (up, hid)):
        out[:, first : first + hid] = sum(
            rows_by_columns(x[...], weight[lax.rem(me[0] + k, n)]) for x, k in pieces
        )


def back_kernel(s, *refs):
    n = len(refs) // 2
    for k in range(n):
        out = refs[n + k]
        out[...] = rows_by_columns(s[...], refs[k][...]).astype(out.dtype)


def acts_kernel(me, far_a, far_b, partial, gate_w, up_w, *refs):
    hidden, grads, x = refs[-3:]
    step = pl.program_id(0)

    @pl.when(step < TILES // 2)
    def _():
        x[...] = far_a[...]

    @pl.when(step >= TILES // 2)
    def _():
        x[...] = far_b[...]

    hid = gate_w.shape[2]
    gate = partial[:, :hid] + rows_by_columns(x[...], gate_w[0])
    upper = partial[:, hid:] + rows_by_columns(x[...], up_w[0])
    back = sum(r[...].astype(F32) for r in refs[:-3])
    sigma = jax.nn.sigmoid(gate)
    active = gate * sigma
    hidden[...] = (active * upper).astype(BF)
    grads[:, :hid] = (back * upper * sigma * (1.0 + gate * (1.0 - sigma))).astype(BF)
    grads[:, hid:] = (back * active).astype(BF)


def dx_kernel(*refs):
    n = len(refs) // 2
    total = mm(refs[0][...], refs[n][...], ((1,), (1,)))
    for k in range(1, n):
        total += mm(refs[k][...], refs[n + k][...], ((1,), (1,)))
    refs[-1][...] = total.astype(BF)


def call(kernel, scalars, ins, outs, grid, scratch, flops, operands):
    moved = sum(a.size * a.dtype.itemsize for a in operands)
    return pl.pallas_call(
        kernel,
        out_shape=[s for s, _ in outs],
        grid_spec=pltpu.PrefetchScalarGridSpec(
            num_scalar_prefetch=scalars,
            grid=grid,
            in_specs=ins,
            out_specs=[b for _, b in outs],
            scratch_shapes=scratch,
        ),
        cost_estimate=pl.CostEstimate(flops=flops, bytes_accessed=moved, transcendentals=0),
    )(*operands)


def per_device(tokens, grad_out, route_ids, route_probs, w_gate, w_up, w_down):
    n_src = lax.axis_size("ep")
    n_tp = lax.axis_size("tp")
    me = lax.axis_index("tp")
    spot = me.astype(jnp.int32).reshape(1)
    tok_rows, quarter = tokens.shape
    top = route_ids.shape[1]
    cap = max(2, 2 * tok_rows * top // n_src)
    rows = n_src * cap
    tile = rows // TILES
    hid = w_gate.shape[2]
    shifts = range(1, n_tp)

    def fetch(a, k):
        return lax.ppermute(a, "tp", [((i + k) % n_tp, i) for i in range(n_tp)])

    def give(a, k):
        return lax.ppermute(a, "tp", [(i, (i + k) % n_tp) for i in range(n_tp)])

    def exchange(a):
        return lax.all_to_all(
            a.reshape(n_src, -1, quarter), "ep", split_axis=0, concat_axis=0, tiled=True
        ).reshape(-1, quarter)

    def by_rows(width):
        return pl.BlockSpec((tile, width), lambda i, *_: (i, 0))

    def whole(shape):
        return pl.BlockSpec(shape, lambda *_: (0,) * len(shape))

    def array(shape, kind):
        return jax.ShapeDtypeStruct(shape, kind)

    ids = route_ids.T
    probs = route_probs.T
    experts = lax.broadcasted_iota(jnp.int32, (n_src, tok_rows), 0)
    hot = [experts == ids[k : k + 1] for k in range(top)]
    named = sum(h.astype(BF) for h in hot)
    before = (
        lax.broadcasted_iota(jnp.int32, (tok_rows, tok_rows), 0)
        < lax.broadcasted_iota(jnp.int32, (tok_rows, tok_rows), 1)
    ).astype(BF)
    earlier = rows_by_columns(named, before)
    ranks = [
        jnp.sum(jnp.where(h, earlier, 0.0), axis=0, keepdims=True).astype(jnp.int32) for h in hot
    ]

    def places(first, count):
        row_index = lax.broadcasted_iota(jnp.int32, (n_src * count, tok_rows), 0)
        at = []
        for k in range(top):
            rank = ranks[k] - first
            inside = (rank >= 0) & (rank < count)
            at.append(row_index == jnp.where(inside, ids[k : k + 1] * count + rank, -1))
        return at

    found = places(0, cap)
    pick = sum(f.astype(BF) for f in found)

    x_own = exchange(rows_by_columns(pick, tokens).astype(BF))
    weight = sum(
        jnp.sum(jnp.where(found[k], probs[k : k + 1], 0.0), axis=1, keepdims=True)
        for k in range(top)
    )
    s_own = exchange((rows_by_columns(pick, grad_out) * weight).astype(BF))

    gate_q = w_gate[0].reshape(n_tp, quarter, hid)
    up_q = w_up[0].reshape(n_tp, quarter, hid)
    down = w_down[0]
    by_span = pl.BlockSpec((n_tp, 128, hid), lambda i, m: (0, i, 0))
    packed = call(
        pack_kernel,
        1,
        [by_span, by_span, whole(down.shape)],
        [(array((quarter, 3 * hid), BF), pl.BlockSpec((128, 3 * hid), lambda i, m: (i, 0)))]
        * n_tp,
        (quarter // 128,),
        [],
        0,
        (spot, gate_q, up_q, down),
    )
    packed = [packed[0]] + [fetch(packed[k], k) for k in shifts]

    half = rows // 2
    x_next, x_last = fetch(x_own, 1), fetch(x_own, n_tp - 1)
    far_a = fetch(x_next[:half], 1)
    far_b = fetch(x_last[half:], n_tp - 1)
    (partial,) = call(
        partial_kernel,
        1,
        [by_rows(quarter)] * 3 + [whole(gate_q.shape), whole(up_q.shape)],
        [(array((rows, 2 * hid), F32), by_rows(2 * hid))],
        (TILES,),
        [],
        12 * rows * quarter * hid,
        (spot, x_own, x_next, x_last, gate_q, up_q),
    )

    terms = call(
        back_kernel,
        0,
        [by_rows(quarter)] + [pl.BlockSpec((quarter, hid), lambda i: (0, 2))] * n_tp,
        [(array((rows, hid), BF if k else F32), by_rows(hid)) for k in range(n_tp)],
        (TILES,),
        [],
        2 * n_tp * rows * quarter * hid,
        (s_own, *packed),
    )
    terms = [terms[0]] + [give(terms[k], k) for k in shifts]
    mid = TILES // 2
    opposite = pl.BlockSpec((1, quarter, hid), lambda i, m: (lax.rem(m[0] + 2, n_tp), 0, 0))
    hidden, d_own = call(
        acts_kernel,
        1,
        [
            pl.BlockSpec((tile, quarter), lambda i, m: (jnp.minimum(i, mid - 1), 0)),
            pl.BlockSpec((tile, quarter), lambda i, m: (jnp.maximum(i - mid, 0), 0)),
            by_rows(2 * hid),
            opposite,
            opposite,
        ]
        + [by_rows(hid)] * n_tp,
        [(array((rows, hid), BF), by_rows(hid)), (array((rows, 2 * hid), BF), by_rows(2 * hid))],
        (TILES,),
        [pltpu.VMEM((tile, quarter), BF)],
        4 * rows * quarter * hid,
        (spot, far_a, far_b, partial, gate_q, up_q, *terms),
    )
    part = cap // CHUNKS
    grad_tokens = 0.0
    for c in range(CHUNKS):
        d_part = d_own.reshape(n_src, cap, 2 * hid)[:, c * part : (c + 1) * part]
        d_part = d_part.reshape(n_src * part, 2 * hid)
        d_all = [d_part] + [fetch(d_part, k) for k in shifts]
        (dx,) = call(
            dx_kernel,
            0,
            [by_rows(2 * hid)] * n_tp
            + [pl.BlockSpec((quarter, 2 * hid), lambda i: (0, 0))] * n_tp,
            [(array((n_src * part, quarter), BF), by_rows(quarter))],
            (TILES // CHUNKS,),
            [],
            4 * n_tp * n_src * part * quarter * hid,
            (*d_all, *packed),
        )
        dx = exchange(dx)
        spots = sum(f.astype(BF) for f in places(c * part, part))
        grad_tokens += mm(spots, dx, ((0,), (0,)))
    grad_tokens = grad_tokens.astype(BF)

    x_full = jnp.zeros((rows, n_tp * quarter), BF)
    x_far = jnp.concatenate([far_a, far_b], axis=0)
    for k, piece in ((0, x_own), (1, x_next), (2, x_far), (n_tp - 1, x_last)):
        start = lax.rem(me + k, n_tp) * quarter
        x_full = lax.dynamic_update_slice_in_dim(x_full, piece, start, axis=1)
    g_gate = mm(x_full, d_own[:, :hid], ((0,), (0,))).astype(BF)
    g_up = mm(x_full, d_own[:, hid:], ((0,), (0,))).astype(BF)

    h_all = [hidden] + [fetch(hidden, k) for k in shifts]
    g_down = jnp.zeros(down.shape, BF)
    for k in range(n_tp):
        piece = mm(h_all[k], s_own, ((0,), (0,))).astype(BF)
        if k:
            piece = give(piece, k)
        start = lax.rem(me + n_tp - k, n_tp) * quarter
        g_down = lax.dynamic_update_slice_in_dim(g_down, piece, start, axis=1)

    return grad_tokens, g_gate[None], g_up[None], g_down[None]


def solution(mesh):
    placed = (
        P("ep", "tp"),
        P("ep", "tp"),
        P("ep", None),
        P("ep", None),
        P("ep", None, "tp"),
        P("ep", None, "tp"),
        P("ep", "tp", None),
    )

    return jax.shard_map(
        per_device,
        mesh=mesh,
        in_specs=placed,
        out_specs=(P("ep", "tp"), P("ep", None, "tp"), P("ep", None, "tp"), P("ep", "tp", None)),
        check_vma=False,
    )
```

```python
import functools

import jax
import jax.numpy as jnp
from jax import lax
from jax.experimental import pallas as pl
from jax.experimental.pallas import tpu as pltpu
from jax.sharding import PartitionSpec as P


TILES = 4
BF = jnp.bfloat16
F32 = jnp.float32


def mm(left, right, dims):
    return lax.dot_general(left, right, (dims, ((), ())), preferred_element_type=F32)


def rows_by_columns(left, right):
    return mm(left, right, ((1,), (0,)))


def pack_kernel(places, me, gate, up, down, *packed):
    step = pl.program_id(0)
    n, span, hid = gate.shape
    width = down.shape[1] // n
    for k, out in zip(places, packed):
        q = lax.rem(me[0] + n - k, n)
        out[:, 0:hid] = gate[q]
        out[:, hid : 2 * hid] = up[q]
        start = pl.multiple_of(q * width + step * span, 128)
        out[:, 2 * hid : 3 * hid] = down[:, pl.ds(start, span)].T


def partial_kernel(me, own, after, last, gate, up, out):
    n, _, hid = gate.shape
    pieces = ((own, 0), (after, 1), (last, n - 1))
    for weight, first in ((gate, 0), (up, hid)):
        out[:, first : first + hid] = sum(
            rows_by_columns(x[...], weight[lax.rem(me[0] + k, n)]) for x, k in pieces
        )


def back_kernel(s, *refs):
    n = len(refs) // 2
    for k in range(n):
        out = refs[n + k]
        out[...] = rows_by_columns(s[...], refs[k][...]).astype(out.dtype)


def acts_kernel(me, far_a, far_b, partial, gate_w, up_w, *refs):
    hidden, grads_a, grads_b, x = refs[-4:]
    step = pl.program_id(0)

    @pl.when(step < TILES // 2)
    def _():
        x[...] = far_a[...]

    @pl.when(step >= TILES // 2)
    def _():
        x[...] = far_b[...]

    hid = gate_w.shape[2]
    gate = partial[:, :hid] + rows_by_columns(x[...], gate_w[0])
    upper = partial[:, hid:] + rows_by_columns(x[...], up_w[0])
    back = sum(r[...].astype(F32) for r in refs[:-4])
    sigma = jax.nn.sigmoid(gate)
    active = gate * sigma
    hidden[...] = (active * upper).astype(BF)
    d_gate = (back * upper * sigma * (1.0 + gate * (1.0 - sigma))).astype(BF)
    d_up = (back * active).astype(BF)

    @pl.when(step < TILES // 2)
    def _():
        grads_a[:, :hid] = d_gate
        grads_a[:, hid:] = d_up

    @pl.when(step >= TILES // 2)
    def _():
        grads_b[:, :hid] = d_gate
        grads_b[:, hid:] = d_up


def dx_kernel(*refs):
    out, d = refs[-2:]
    n = (len(refs) - 2) // 3
    width = refs[0].shape[1]
    step = pl.program_id(0)

    @pl.when(step < TILES // 2)
    def _():
        for k in range(n):
            d[:, k * width : (k + 1) * width] = refs[k][...]

    @pl.when(step >= TILES // 2)
    def _():
        for k in range(n):
            d[:, k * width : (k + 1) * width] = refs[n + k][...]

    out[...] = sum(
        mm(d[:, k * width : (k + 1) * width], refs[2 * n + k][...], ((1,), (1,))) for k in range(n)
    ).astype(BF)


def call(kernel, scalars, ins, outs, grid, scratch, flops, operands):
    moved = sum(a.size * a.dtype.itemsize for a in operands)
    return pl.pallas_call(
        kernel,
        out_shape=[s for s, _ in outs],
        grid_spec=pltpu.PrefetchScalarGridSpec(
            num_scalar_prefetch=scalars,
            grid=grid,
            in_specs=ins,
            out_specs=[b for _, b in outs],
            scratch_shapes=scratch,
        ),
        cost_estimate=pl.CostEstimate(flops=flops, bytes_accessed=moved, transcendentals=0),
    )(*operands)


def per_device(tokens, grad_out, route_ids, route_probs, w_gate, w_up, w_down):
    n_src = lax.axis_size("ep")
    n_tp = lax.axis_size("tp")
    me = lax.axis_index("tp")
    spot = me.astype(jnp.int32).reshape(1)
    tok_rows, quarter = tokens.shape
    top = route_ids.shape[1]
    cap = max(2, 2 * tok_rows * top // n_src)
    rows = n_src * cap
    tile = rows // TILES
    hid = w_gate.shape[2]
    shifts = range(1, n_tp)

    def fetch(a, k):
        return lax.ppermute(a, "tp", [((i + k) % n_tp, i) for i in range(n_tp)])

    def give(a, k):
        return lax.ppermute(a, "tp", [(i, (i + k) % n_tp) for i in range(n_tp)])

    def exchange(a):
        return lax.all_to_all(
            a.reshape(n_src, -1, quarter), "ep", split_axis=0, concat_axis=0, tiled=True
        ).reshape(-1, quarter)

    def by_rows(width):
        return pl.BlockSpec((tile, width), lambda i, *_: (i, 0))

    def whole(shape):
        return pl.BlockSpec(shape, lambda *_: (0,) * len(shape))

    def array(shape, kind):
        return jax.ShapeDtypeStruct(shape, kind)

    ids = route_ids.T
    probs = route_probs.T
    experts = lax.broadcasted_iota(jnp.int32, (n_src, tok_rows), 0)
    hot = [experts == ids[k : k + 1] for k in range(top)]
    named = sum(h.astype(BF) for h in hot)
    before = (
        lax.broadcasted_iota(jnp.int32, (tok_rows, tok_rows), 0)
        < lax.broadcasted_iota(jnp.int32, (tok_rows, tok_rows), 1)
    ).astype(BF)
    earlier = rows_by_columns(named, before)
    ranks = [
        jnp.sum(jnp.where(h, earlier, 0.0), axis=0, keepdims=True).astype(jnp.int32) for h in hot
    ]

    row_index = lax.broadcasted_iota(jnp.int32, (rows, tok_rows), 0)
    found = [row_index == ids[k : k + 1] * cap + ranks[k] for k in range(top)]
    pick = sum(f.astype(BF) for f in found)

    x_own = exchange(rows_by_columns(pick, tokens).astype(BF))
    weight = sum(
        jnp.sum(jnp.where(found[k], probs[k : k + 1], 0.0), axis=1, keepdims=True)
        for k in range(top)
    )
    s_own = exchange((rows_by_columns(pick, grad_out) * weight).astype(BF))

    gate_q = w_gate[0].reshape(n_tp, quarter, hid)
    up_q = w_up[0].reshape(n_tp, quarter, hid)
    down = w_down[0]
    by_span = pl.BlockSpec((n_tp, 128, hid), lambda i, m: (0, i, 0))

    def pack(places):
        return call(
            functools.partial(pack_kernel, places),
            1,
            [by_span, by_span, whole(down.shape)],
            [(array((quarter, 3 * hid), BF), pl.BlockSpec((128, 3 * hid), lambda i, m: (i, 0)))]
            * len(places),
            (quarter // 128,),
            [],
            0,
            (spot, gate_q, up_q, down),
        )

    sent = pack(tuple(shifts))
    packed = list(pack((0,))) + [fetch(sent[k - 1], k) for k in shifts]

    half = rows // 2
    x_next, x_last = fetch(x_own, 1), fetch(x_own, n_tp - 1)
    far_a = fetch(x_next[:half], 1)
    far_b = fetch(x_last[half:], n_tp - 1)
    (partial,) = call(
        partial_kernel,
        1,
        [by_rows(quarter)] * 3 + [whole(gate_q.shape), whole(up_q.shape)],
        [(array((rows, 2 * hid), F32), by_rows(2 * hid))],
        (TILES,),
        [],
        12 * rows * quarter * hid,
        (spot, x_own, x_next, x_last, gate_q, up_q),
    )

    terms = call(
        back_kernel,
        0,
        [by_rows(quarter)] + [pl.BlockSpec((quarter, hid), lambda i: (0, 2))] * n_tp,
        [(array((rows, hid), BF if k else F32), by_rows(hid)) for k in range(n_tp)],
        (TILES,),
        [],
        2 * n_tp * rows * quarter * hid,
        (s_own, *packed),
    )
    terms = [terms[0]] + [give(terms[k], k) for k in shifts]
    mid = TILES // 2

    def upper_rows(width):
        return pl.BlockSpec((tile, width), lambda i, *_: (jnp.minimum(i, mid - 1), 0))

    def lower_rows(width):
        return pl.BlockSpec((tile, width), lambda i, *_: (jnp.maximum(i - mid, 0), 0))

    opposite = pl.BlockSpec((1, quarter, hid), lambda i, m: (lax.rem(m[0] + 2, n_tp), 0, 0))
    hidden, d_a, d_b = call(
        acts_kernel,
        1,
        [
            upper_rows(quarter),
            lower_rows(quarter),
            by_rows(2 * hid),
            opposite,
            opposite,
        ]
        + [by_rows(hid)] * n_tp,
        [
            (array((rows, hid), BF), by_rows(hid)),
            (array((half, 2 * hid), BF), upper_rows(2 * hid)),
            (array((half, 2 * hid), BF), lower_rows(2 * hid)),
        ],
        (TILES,),
        [pltpu.VMEM((tile, quarter), BF)],
        4 * rows * quarter * hid,
        (spot, far_a, far_b, partial, gate_q, up_q, *terms),
    )
    back_one = n_tp - 1
    next_a, last_b = fetch(d_a, 1), fetch(d_b, back_one)
    next_b, last_a = fetch(d_b, 1), fetch(d_a, back_one)
    passed_a, passed_b = fetch(next_a, 1), fetch(last_b, back_one)
    halves = (d_a, next_a, passed_a, last_a, d_b, next_b, passed_b, last_b)
    (dx,) = call(
        dx_kernel,
        0,
        [upper_rows(2 * hid)] * n_tp
        + [lower_rows(2 * hid)] * n_tp
        + [pl.BlockSpec((quarter, 2 * hid), lambda i: (0, 0))] * n_tp,
        [(array((rows, quarter), BF), by_rows(quarter))],
        (TILES,),
        [pltpu.VMEM((tile, 2 * hid * n_tp), BF)],
        4 * n_tp * rows * quarter * hid,
        (*halves, *packed),
    )
    dx = exchange(dx)
    grad_tokens = mm(pick, dx, ((0,), (0,))).astype(BF)

    x_full = jnp.zeros((rows, n_tp * quarter), BF)
    x_far = jnp.concatenate([far_a, far_b], axis=0)
    for k, piece in ((0, x_own), (1, x_next), (2, x_far), (n_tp - 1, x_last)):
        start = lax.rem(me + k, n_tp) * quarter
        x_full = lax.dynamic_update_slice_in_dim(x_full, piece, start, axis=1)
    d_own = jnp.concatenate([d_a, d_b], axis=0)
    g_gate = mm(x_full, d_own[:, :hid], ((0,), (0,))).astype(BF)
    g_up = mm(x_full, d_own[:, hid:], ((0,), (0,))).astype(BF)

    h_all = [hidden] + [fetch(hidden, k) for k in shifts]
    g_down = jnp.zeros(down.shape, BF)
    for k in range(n_tp):
        piece = mm(h_all[k], s_own, ((0,), (0,))).astype(BF)
        if k:
            piece = give(piece, k)
        start = lax.rem(me + n_tp - k, n_tp) * quarter
        g_down = lax.dynamic_update_slice_in_dim(g_down, piece, start, axis=1)

    return grad_tokens, g_gate[None], g_up[None], g_down[None]


def solution(mesh):
    placed = (
        P("ep", "tp"),
        P("ep", "tp"),
        P("ep", None),
        P("ep", None),
        P("ep", None, "tp"),
        P("ep", None, "tp"),
        P("ep", "tp", None),
    )

    return jax.shard_map(
        per_device,
        mesh=mesh,
        in_specs=placed,
        out_specs=(P("ep", "tp"), P("ep", None, "tp"), P("ep", None, "tp"), P("ep", "tp", None)),
        check_vma=False,
    )
```

```python
import functools

import jax
import jax.numpy as jnp
from jax import lax
from jax.experimental import pallas as pl
from jax.experimental.pallas import tpu as pltpu
from jax.sharding import PartitionSpec as P


TILES = 4
BF = jnp.bfloat16
F32 = jnp.float32


def mm(left, right, dims):
    return lax.dot_general(left, right, (dims, ((), ())), preferred_element_type=F32)


def rows_by_columns(left, right):
    return mm(left, right, ((1,), (0,)))


def pack_kernel(places, me, gate, up, down, *packed):
    step = pl.program_id(0)
    n, span, hid = gate.shape
    width = down.shape[1] // n
    rows, columns = (lax.broadcasted_iota(jnp.int32, (span, span), d) for d in (0, 1))
    same = (rows == columns).astype(BF)
    for k, out in zip(places, packed):
        q = lax.rem(me[0] + n - k, n)
        out[:, 0:hid] = gate[q]
        out[:, hid : 2 * hid] = up[q]
        start = pl.multiple_of(q * width + step * span, 128)
        turned = mm(same, down[:, pl.ds(start, span)], ((1,), (1,)))
        out[:, 2 * hid : 3 * hid] = turned.astype(BF)


def partial_kernel(me, own, after, last, gate, up, out):
    n, _, hid = gate.shape
    pieces = ((own, 0), (after, 1), (last, n - 1))
    for weight, first in ((gate, 0), (up, hid)):
        out[:, first : first + hid] = sum(
            rows_by_columns(x[...], weight[lax.rem(me[0] + k, n)]) for x, k in pieces
        )


def back_kernel(s, *refs):
    n = len(refs) // 2
    for k in range(n):
        out = refs[n + k]
        out[...] = rows_by_columns(s[...], refs[k][...]).astype(out.dtype)


def acts_kernel(me, far_a, far_b, partial, gate_w, up_w, *refs):
    hidden, grads_a, grads_b, x = refs[-4:]
    step = pl.program_id(0)

    @pl.when(step < TILES // 2)
    def _():
        x[...] = far_a[...]

    @pl.when(step >= TILES // 2)
    def _():
        x[...] = far_b[...]

    hid = gate_w.shape[2]
    gate = partial[:, :hid] + rows_by_columns(x[...], gate_w[0])
    upper = partial[:, hid:] + rows_by_columns(x[...], up_w[0])
    back = sum(r[...].astype(F32) for r in refs[:-4])
    sigma = jax.nn.sigmoid(gate)
    active = gate * sigma
    hidden[...] = (active * upper).astype(BF)
    d_gate = (back * upper * sigma * (1.0 + gate * (1.0 - sigma))).astype(BF)
    d_up = (back * active).astype(BF)

    @pl.when(step < TILES // 2)
    def _():
        grads_a[:, :hid] = d_gate
        grads_a[:, hid:] = d_up

    @pl.when(step >= TILES // 2)
    def _():
        grads_b[:, :hid] = d_gate
        grads_b[:, hid:] = d_up


def dx_kernel(n, *refs):
    out, d = refs[-2:]
    width = refs[0].shape[1]
    step = pl.program_id(0)

    @pl.when(step < TILES // 2)
    def _():
        for k in range(n):
            d[:, k * width : (k + 1) * width] = refs[k][...]

    @pl.when(step >= TILES // 2)
    def _():
        for k in range(n):
            d[:, k * width : (k + 1) * width] = refs[n + k][...]

    total = sum(
        mm(d[:, k * width : (k + 1) * width], refs[2 * n + k][...], ((1,), (1,))) for k in range(n)
    )
    for so_far in refs[3 * n : -2]:
        total += so_far[...]
    out[...] = total.astype(out.dtype)


def call(kernel, scalars, ins, outs, grid, scratch, flops, operands):
    moved = sum(a.size * a.dtype.itemsize for a in operands)
    return pl.pallas_call(
        kernel,
        out_shape=[s for s, _ in outs],
        grid_spec=pltpu.PrefetchScalarGridSpec(
            num_scalar_prefetch=scalars,
            grid=grid,
            in_specs=ins,
            out_specs=[b for _, b in outs],
            scratch_shapes=scratch,
        ),
        cost_estimate=pl.CostEstimate(flops=flops, bytes_accessed=moved, transcendentals=0),
    )(*operands)


def per_device(tokens, grad_out, route_ids, route_probs, w_gate, w_up, w_down):
    n_src = lax.axis_size("ep")
    n_tp = lax.axis_size("tp")
    me = lax.axis_index("tp")
    spot = me.astype(jnp.int32).reshape(1)
    tok_rows, quarter = tokens.shape
    top = route_ids.shape[1]
    cap = max(2, 2 * tok_rows * top // n_src)
    rows = n_src * cap
    tile = rows // TILES
    hid = w_gate.shape[2]
    shifts = range(1, n_tp)

    def fetch(a, k):
        return lax.ppermute(a, "tp", [((i + k) % n_tp, i) for i in range(n_tp)])

    def give(a, k):
        return lax.ppermute(a, "tp", [(i, (i + k) % n_tp) for i in range(n_tp)])

    def exchange(a):
        return lax.all_to_all(
            a.reshape(n_src, -1, quarter), "ep", split_axis=0, concat_axis=0, tiled=True
        ).reshape(-1, quarter)

    def by_rows(width):
        return pl.BlockSpec((tile, width), lambda i, *_: (i, 0))

    def whole(shape):
        return pl.BlockSpec(shape, lambda *_: (0,) * len(shape))

    def array(shape, kind):
        return jax.ShapeDtypeStruct(shape, kind)

    ids = route_ids.T
    probs = route_probs.T
    experts = lax.broadcasted_iota(jnp.int32, (n_src, tok_rows), 0)
    hot = [experts == ids[k : k + 1] for k in range(top)]
    named = sum(h.astype(BF) for h in hot)
    before = (
        lax.broadcasted_iota(jnp.int32, (tok_rows, tok_rows), 0)
        < lax.broadcasted_iota(jnp.int32, (tok_rows, tok_rows), 1)
    ).astype(BF)
    earlier = rows_by_columns(named, before)
    ranks = [
        jnp.sum(jnp.where(h, earlier, 0.0), axis=0, keepdims=True).astype(jnp.int32) for h in hot
    ]

    row_index = lax.broadcasted_iota(jnp.int32, (rows, tok_rows), 0)
    found = [row_index == ids[k : k + 1] * cap + ranks[k] for k in range(top)]
    pick = sum(f.astype(BF) for f in found)

    x_own = exchange(rows_by_columns(pick, tokens).astype(BF))
    weight = sum(
        jnp.sum(jnp.where(found[k], probs[k : k + 1], 0.0), axis=1, keepdims=True)
        for k in range(top)
    )
    s_own = exchange((rows_by_columns(pick, grad_out) * weight).astype(BF))

    gate_q = w_gate[0].reshape(n_tp, quarter, hid)
    up_q = w_up[0].reshape(n_tp, quarter, hid)
    down = w_down[0]
    by_span = pl.BlockSpec((n_tp, 128, hid), lambda i, m: (0, i, 0))

    def pack(places):
        return call(
            functools.partial(pack_kernel, places),
            1,
            [by_span, by_span, whole(down.shape)],
            [(array((quarter, 3 * hid), BF), pl.BlockSpec((128, 3 * hid), lambda i, m: (i, 0)))]
            * len(places),
            (quarter // 128,),
            [],
            0,
            (spot, gate_q, up_q, down),
        )

    sent = pack(tuple(shifts))
    packed = list(pack((0,))) + [fetch(sent[k - 1], k) for k in shifts]

    half = rows // 2
    x_next, x_last = fetch(x_own, 1), fetch(x_own, n_tp - 1)
    far_a = fetch(x_next[:half], 1)
    far_b = fetch(x_last[half:], n_tp - 1)
    (partial,) = call(
        partial_kernel,
        1,
        [by_rows(quarter)] * 3 + [whole(gate_q.shape), whole(up_q.shape)],
        [(array((rows, 2 * hid), F32), by_rows(2 * hid))],
        (TILES,),
        [],
        12 * rows * quarter * hid,
        (spot, x_own, x_next, x_last, gate_q, up_q),
    )

    terms = call(
        back_kernel,
        0,
        [by_rows(quarter)] + [pl.BlockSpec((quarter, hid), lambda i: (0, 2))] * n_tp,
        [(array((rows, hid), BF if k else F32), by_rows(hid)) for k in range(n_tp)],
        (TILES,),
        [],
        2 * n_tp * rows * quarter * hid,
        (s_own, *packed),
    )
    terms = [terms[0]] + [give(terms[k], k) for k in shifts]
    mid = TILES // 2

    def upper_rows(width):
        return pl.BlockSpec((tile, width), lambda i, *_: (jnp.minimum(i, mid - 1), 0))

    def lower_rows(width):
        return pl.BlockSpec((tile, width), lambda i, *_: (jnp.maximum(i - mid, 0), 0))

    opposite = pl.BlockSpec((1, quarter, hid), lambda i, m: (lax.rem(m[0] + 2, n_tp), 0, 0))
    hidden, d_a, d_b = call(
        acts_kernel,
        1,
        [
            upper_rows(quarter),
            lower_rows(quarter),
            by_rows(2 * hid),
            opposite,
            opposite,
        ]
        + [by_rows(hid)] * n_tp,
        [
            (array((rows, hid), BF), by_rows(hid)),
            (array((half, 2 * hid), BF), upper_rows(2 * hid)),
            (array((half, 2 * hid), BF), lower_rows(2 * hid)),
        ],
        (TILES,),
        [pltpu.VMEM((tile, quarter), BF)],
        4 * rows * quarter * hid,
        (spot, far_a, far_b, partial, gate_q, up_q, *terms),
    )
    back_one = n_tp - 1
    next_a, last_b = fetch(d_a, 1), fetch(d_b, back_one)
    next_b, last_a = fetch(d_b, 1), fetch(d_a, back_one)
    passed_a, passed_b = fetch(next_a, 1), fetch(last_b, back_one)

    def add_up(upper, lower, weights, so_far, kind):
        n = len(upper)
        return call(
            functools.partial(dx_kernel, n),
            0,
            [upper_rows(2 * hid)] * n
            + [lower_rows(2 * hid)] * n
            + [pl.BlockSpec((quarter, 2 * hid), lambda i: (0, 0))] * n
            + [by_rows(quarter)] * len(so_far),
            [(array((rows, quarter), kind), by_rows(quarter))],
            (TILES,),
            [pltpu.VMEM((tile, 2 * hid * n), BF)],
            4 * n * rows * quarter * hid,
            (*upper, *lower, *weights, *so_far),
        )

    near = (packed[0], packed[1], packed[back_one])
    so_far = add_up((d_a, next_a, last_a), (d_b, next_b, last_b), near, (), F32)
    (dx,) = add_up((passed_a,), (passed_b,), (packed[2],), so_far, BF)
    dx = exchange(dx)
    grad_tokens = mm(pick, dx, ((0,), (0,))).astype(BF)

    x_full = jnp.zeros((rows, n_tp * quarter), BF)
    x_far = jnp.concatenate([far_a, far_b], axis=0)
    for k, piece in ((0, x_own), (1, x_next), (2, x_far), (n_tp - 1, x_last)):
        start = lax.rem(me + k, n_tp) * quarter
        x_full = lax.dynamic_update_slice_in_dim(x_full, piece, start, axis=1)
    d_own = jnp.concatenate([d_a, d_b], axis=0)
    g_gate = mm(x_full, d_own[:, :hid], ((0,), (0,))).astype(BF)
    g_up = mm(x_full, d_own[:, hid:], ((0,), (0,))).astype(BF)

    h_all = [hidden] + [fetch(hidden, k) for k in shifts]
    g_down = jnp.zeros(down.shape, BF)
    for k in range(n_tp):
        piece = mm(h_all[k], s_own, ((0,), (0,))).astype(BF)
        if k:
            piece = give(piece, k)
        start = lax.rem(me + n_tp - k, n_tp) * quarter
        g_down = lax.dynamic_update_slice_in_dim(g_down, piece, start, axis=1)

    return grad_tokens, g_gate[None], g_up[None], g_down[None]


def solution(mesh):
    placed = (
        P("ep", "tp"),
        P("ep", "tp"),
        P("ep", None),
        P("ep", None),
        P("ep", None, "tp"),
        P("ep", None, "tp"),
        P("ep", "tp", None),
    )

    return jax.shard_map(
        per_device,
        mesh=mesh,
        in_specs=placed,
        out_specs=(P("ep", "tp"), P("ep", None, "tp"), P("ep", None, "tp"), P("ep", "tp", None)),
        check_vma=False,
    )
```

```python
import functools

import jax
import jax.numpy as jnp
from jax import lax
from jax.experimental import pallas as pl
from jax.experimental.pallas import tpu as pltpu
from jax.sharding import PartitionSpec as P


TILES = 4
BF = jnp.bfloat16
F32 = jnp.float32


def mm(left, right, dims):
    return lax.dot_general(left, right, (dims, ((), ())), preferred_element_type=F32)


def rows_by_columns(left, right):
    return mm(left, right, ((1,), (0,)))


def pack_kernel(places, me, gate, up, down, *packed):
    step = pl.program_id(0)
    n, span, hid = gate.shape
    width = down.shape[1] // n
    for k, out in zip(places, packed):
        q = lax.rem(me[0] + n - k, n)
        out[:, 0:hid] = gate[q]
        out[:, hid : 2 * hid] = up[q]
        start = pl.multiple_of(q * width + step * span, 128)
        out[:, 2 * hid : 3 * hid] = down[:, pl.ds(start, span)].T


def partial_kernel(me, own, after, last, gate, up, out):
    n, _, hid = gate.shape
    pieces = ((own, 0), (after, 1), (last, n - 1))
    for weight, first in ((gate, 0), (up, hid)):
        out[:, first : first + hid] = sum(
            rows_by_columns(x[...], weight[lax.rem(me[0] + k, n)]) for x, k in pieces
        )


def back_kernel(s, *refs):
    n = len(refs) // 2
    for k in range(n):
        out = refs[n + k]
        out[...] = rows_by_columns(s[...], refs[k][...]).astype(out.dtype)


def acts_kernel(me, far_a, far_b, partial, gate_w, up_w, *refs):
    hidden, grads_a, grads_b, x = refs[-4:]
    step = pl.program_id(0)

    @pl.when(step < TILES // 2)
    def _():
        x[...] = far_a[...]

    @pl.when(step >= TILES // 2)
    def _():
        x[...] = far_b[...]

    hid = gate_w.shape[2]
    gate = partial[:, :hid] + rows_by_columns(x[...], gate_w[0])
    upper = partial[:, hid:] + rows_by_columns(x[...], up_w[0])
    back = sum(r[...].astype(F32) for r in refs[:-4])
    sigma = jax.nn.sigmoid(gate)
    active = gate * sigma
    hidden[...] = (active * upper).astype(BF)
    d_gate = (back * upper * sigma * (1.0 + gate * (1.0 - sigma))).astype(BF)
    d_up = (back * active).astype(BF)

    @pl.when(step < TILES // 2)
    def _():
        grads_a[:, :hid] = d_gate
        grads_a[:, hid:] = d_up

    @pl.when(step >= TILES // 2)
    def _():
        grads_b[:, :hid] = d_gate
        grads_b[:, hid:] = d_up


def dx_kernel(n, *refs):
    out, d = refs[-2:]
    width = refs[0].shape[1]
    step = pl.program_id(0)

    @pl.when(step < TILES // 2)
    def _():
        for k in range(n):
            d[:, k * width : (k + 1) * width] = refs[k][...]

    @pl.when(step >= TILES // 2)
    def _():
        for k in range(n):
            d[:, k * width : (k + 1) * width] = refs[n + k][...]

    total = sum(
        mm(d[:, k * width : (k + 1) * width], refs[2 * n + k][...], ((1,), (1,))) for k in range(n)
    )
    for so_far in refs[3 * n : -2]:
        total += so_far[...]
    out[...] = total.astype(out.dtype)


def call(kernel, scalars, ins, outs, grid, scratch, flops, operands):
    moved = sum(a.size * a.dtype.itemsize for a in operands)
    return pl.pallas_call(
        kernel,
        out_shape=[s for s, _ in outs],
        grid_spec=pltpu.PrefetchScalarGridSpec(
            num_scalar_prefetch=scalars,
            grid=grid,
            in_specs=ins,
            out_specs=[b for _, b in outs],
            scratch_shapes=scratch,
        ),
        cost_estimate=pl.CostEstimate(flops=flops, bytes_accessed=moved, transcendentals=0),
    )(*operands)


def per_device(tokens, grad_out, route_ids, route_probs, w_gate, w_up, w_down):
    n_src = lax.axis_size("ep")
    n_tp = lax.axis_size("tp")
    me = lax.axis_index("tp")
    spot = me.astype(jnp.int32).reshape(1)
    tok_rows, quarter = tokens.shape
    top = route_ids.shape[1]
    cap = max(2, 2 * tok_rows * top // n_src)
    rows = n_src * cap
    tile = rows // TILES
    hid = w_gate.shape[2]
    shifts = range(1, n_tp)

    def fetch(a, k):
        return lax.ppermute(a, "tp", [((i + k) % n_tp, i) for i in range(n_tp)])

    def give(a, k):
        return lax.ppermute(a, "tp", [(i, (i + k) % n_tp) for i in range(n_tp)])

    def exchange(a):
        return lax.all_to_all(
            a.reshape(n_src, -1, quarter), "ep", split_axis=0, concat_axis=0, tiled=True
        ).reshape(-1, quarter)

    def by_rows(width):
        return pl.BlockSpec((tile, width), lambda i, *_: (i, 0))

    def whole(shape):
        return pl.BlockSpec(shape, lambda *_: (0,) * len(shape))

    def array(shape, kind):
        return jax.ShapeDtypeStruct(shape, kind)

    ids = route_ids.T
    probs = route_probs.T
    experts = lax.broadcasted_iota(jnp.int32, (n_src, tok_rows), 0)
    hot = [experts == ids[k : k + 1] for k in range(top)]
    named = sum(h.astype(BF) for h in hot)
    before = (
        lax.broadcasted_iota(jnp.int32, (tok_rows, tok_rows), 0)
        < lax.broadcasted_iota(jnp.int32, (tok_rows, tok_rows), 1)
    ).astype(BF)
    earlier = rows_by_columns(named, before)
    ranks = [
        jnp.sum(jnp.where(h, earlier, 0.0), axis=0, keepdims=True).astype(jnp.int32) for h in hot
    ]

    row_index = lax.broadcasted_iota(jnp.int32, (rows, tok_rows), 0)
    found = [row_index == ids[k : k + 1] * cap + ranks[k] for k in range(top)]
    pick = sum(f.astype(BF) for f in found)

    x_own = exchange(rows_by_columns(pick, tokens).astype(BF))
    weight = sum(
        jnp.sum(jnp.where(found[k], probs[k : k + 1], 0.0), axis=1, keepdims=True)
        for k in range(top)
    )
    s_own = exchange((rows_by_columns(pick, grad_out) * weight).astype(BF))

    gate_q = w_gate[0].reshape(n_tp, quarter, hid)
    up_q = w_up[0].reshape(n_tp, quarter, hid)
    down = w_down[0]
    by_span = pl.BlockSpec((n_tp, 128, hid), lambda i, m: (0, i, 0))

    def pack(places):
        return call(
            functools.partial(pack_kernel, places),
            1,
            [by_span, by_span, whole(down.shape)],
            [(array((quarter, 3 * hid), BF), pl.BlockSpec((128, 3 * hid), lambda i, m: (i, 0)))]
            * len(places),
            (quarter // 128,),
            [],
            0,
            (spot, gate_q, up_q, down),
        )

    sent = pack(tuple(shifts))
    packed = list(pack((0,))) + [fetch(sent[k - 1], k) for k in shifts]

    half = rows // 2
    x_next, x_last = fetch(x_own, 1), fetch(x_own, n_tp - 1)
    far_a = fetch(x_next[:half], 1)
    far_b = fetch(x_last[half:], n_tp - 1)
    (partial,) = call(
        partial_kernel,
        1,
        [by_rows(quarter)] * 3 + [whole(gate_q.shape), whole(up_q.shape)],
        [(array((rows, 2 * hid), F32), by_rows(2 * hid))],
        (TILES,),
        [],
        12 * rows * quarter * hid,
        (spot, x_own, x_next, x_last, gate_q, up_q),
    )

    terms = call(
        back_kernel,
        0,
        [by_rows(quarter)] + [pl.BlockSpec((quarter, hid), lambda i: (0, 2))] * n_tp,
        [(array((rows, hid), BF if k else F32), by_rows(hid)) for k in range(n_tp)],
        (TILES,),
        [],
        2 * n_tp * rows * quarter * hid,
        (s_own, *packed),
    )
    terms = [terms[0]] + [give(terms[k], k) for k in shifts]
    mid = TILES // 2

    def upper_rows(width):
        return pl.BlockSpec((tile, width), lambda i, *_: (jnp.minimum(i, mid - 1), 0))

    def lower_rows(width):
        return pl.BlockSpec((tile, width), lambda i, *_: (jnp.maximum(i - mid, 0), 0))

    opposite = pl.BlockSpec((1, quarter, hid), lambda i, m: (lax.rem(m[0] + 2, n_tp), 0, 0))
    hidden, d_a, d_b = call(
        acts_kernel,
        1,
        [
            upper_rows(quarter),
            lower_rows(quarter),
            by_rows(2 * hid),
            opposite,
            opposite,
        ]
        + [by_rows(hid)] * n_tp,
        [
            (array((rows, hid), BF), by_rows(hid)),
            (array((half, 2 * hid), BF), upper_rows(2 * hid)),
            (array((half, 2 * hid), BF), lower_rows(2 * hid)),
        ],
        (TILES,),
        [pltpu.VMEM((tile, quarter), BF)],
        4 * rows * quarter * hid,
        (spot, far_a, far_b, partial, gate_q, up_q, *terms),
    )
    back_one = n_tp - 1
    next_a, last_b = fetch(d_a, 1), fetch(d_b, back_one)
    next_b, last_a = fetch(d_b, 1), fetch(d_a, back_one)
    passed_a, passed_b = fetch(next_a, 1), fetch(last_b, back_one)

    def add_up(upper, lower, weights, so_far, kind):
        n = len(upper)
        return call(
            functools.partial(dx_kernel, n),
            0,
            [upper_rows(2 * hid)] * n
            + [lower_rows(2 * hid)] * n
            + [pl.BlockSpec((quarter, 2 * hid), lambda i: (0, 0))] * n
            + [by_rows(quarter)] * len(so_far),
            [(array((rows, quarter), kind), by_rows(quarter))],
            (TILES,),
            [pltpu.VMEM((tile, 2 * hid * n), BF)],
            4 * n * rows * quarter * hid,
            (*upper, *lower, *weights, *so_far),
        )

    near = (packed[0], packed[1], packed[back_one])
    so_far = add_up((d_a, next_a, last_a), (d_b, next_b, last_b), near, (), F32)
    (dx,) = add_up((passed_a,), (passed_b,), (packed[2],), so_far, BF)
    dx = exchange(dx)
    grad_tokens = mm(pick, dx, ((0,), (0,))).astype(BF)

    x_full = jnp.zeros((rows, n_tp * quarter), BF)
    x_far = jnp.concatenate([far_a, far_b], axis=0)
    for k, piece in ((0, x_own), (1, x_next), (2, x_far), (n_tp - 1, x_last)):
        start = lax.rem(me + k, n_tp) * quarter
        x_full = lax.dynamic_update_slice_in_dim(x_full, piece, start, axis=1)
    d_own = jnp.concatenate([d_a, d_b], axis=0)
    g_gate = mm(x_full, d_own[:, :hid], ((0,), (0,))).astype(BF)
    g_up = mm(x_full, d_own[:, hid:], ((0,), (0,))).astype(BF)

    h_all = [hidden] + [fetch(hidden, k) for k in shifts]
    g_down = jnp.zeros(down.shape, BF)
    for k in range(n_tp):
        piece = mm(h_all[k], s_own, ((0,), (0,))).astype(BF)
        if k:
            piece = give(piece, k)
        start = lax.rem(me + n_tp - k, n_tp) * quarter
        g_down = lax.dynamic_update_slice_in_dim(g_down, piece, start, axis=1)

    return grad_tokens, g_gate[None], g_up[None], g_down[None]


def solution(mesh):
    placed = (
        P("ep", "tp"),
        P("ep", "tp"),
        P("ep", None),
        P("ep", None),
        P("ep", None, "tp"),
        P("ep", None, "tp"),
        P("ep", "tp", None),
    )

    return jax.shard_map(
        per_device,
        mesh=mesh,
        in_specs=placed,
        out_specs=(P("ep", "tp"), P("ep", None, "tp"), P("ep", None, "tp"), P("ep", "tp", None)),
        check_vma=False,
    )
```
